32 devices in a mesh: group: 2 (over x), tile: 16 (over z, y, core).
Axes of the slice: x: 2, y: 2, z: 4, core: 2. Of those that a mesh axis runs over, the one named last changes fastest.
Arguments:
- latents: bfloat16 [384, 16, 128], P(('group', 'tile')), parts along dimension 0, may hold values from -6 to 6
- clip_index: int32 [8], P('group'), parts along dimension 0, may hold values from 0 to 1, never falling along the last dimension, each value on 1 to 3 neighbouring positions
- first_conv: bfloat16 [3, 3, 3, 16, 384], replicated, may hold values from -0.3125 to 0.3125
- first_gain: float32 [384], replicated, may hold values from 0.4 to 1.6
- middle_conv: bfloat16 [3, 3, 3, 384, 384], replicated, may hold values from -0.0625 to 0.0625
- head_gain: float32 [384], replicated, may hold values from 0.4 to 1.6
- head_weight: bfloat16 [384, 48], replicated, may hold values from -0.3125 to 0.3125
Outputs:
- pixels: float32 [32, 2, 3, 48, 128], P(('group', 'tile')), parts along dimension 0
The draws below stay inside these ranges and needn't reach their ends.
There are 2 independent parts, one for each index of `group`. The reference program is written for one: setup_inputs(seed, part) draws one part's arguments, and reference() takes and returns one part's arrays. A program takes and returns all parts, laid end to end along the dimension named above; an argument that names none is the same for every part. Nothing has to cross between parts.
Inputs may be any that keep to these rules, and one draw needn't show every extreme that they name: `clip_index`: clip numbers never fall along the frames; each clip holds 1 to 3 consecutive frames.
All inputs are finite; a program needn't handle non-finite values.
Results may differ from the reference program's by a relative error of at most 0.01.
Values may be sent and summed in bfloat16 or wider, within the bound.
A program may use at most 128 MiB of HBM per device.

```python
import math
import jax
import jax.numpy as jnp
import numpy as np
from jax import lax

CLAT = 16
CH = 384
PATCH = 16
STRIPS = 8
TF = 2
WS = 16
HL = 48
BLOCKS = 2
TILES = 16
FRAMES = 4
WL = 128
CLIPS = 2
CLIP_MOST = 3


def block_levels(rng, extent, pieces, smallest, top_value):
    def one(axis_at, shards_of):
        draws = jax.random.uniform(jax.random.fold_in(jax.random.fold_in(rng, 6), axis_at), (shards_of,), jnp.float32, smallest / len(pieces), top_value / len(pieces))
        return jnp.repeat(jnp.exp(draws), extent[axis_at] // shards_of).reshape((-1,) + (1,) * (len(extent) - axis_at - 1))

    loudness = one(*pieces[0])
    for cut in pieces[1:]:
        loudness = loudness * one(*cut)
    return loudness


def profile(count, total, most, slope):
    portions = [(1 << 20) // math.isqrt(standing ** slope) + 1 for standing in range(2, count + 1)]
    spare, counts = total - most - (count - 1), [1] * (count - 1)
    while spare > 0:
        candidates = [i for i in range(count - 1) if counts[i] < most]
        pool, left = sum([portions[i] for i in candidates]), spare
        for i in candidates:
            more = min(most - counts[i], max(1, left * portions[i] // pool), spare)
            counts[i] = counts[i] + more
            spare = spare - more
    return np.array([most] + counts)


def uneven_parts(own_key, count, total, most, skew):
    if count == 2:
        one = jax.random.randint(own_key, (), max(1, total - most), min(most, total - 1) + 1)
        return jnp.stack([one, total - one])
    tallies = jnp.asarray(profile(count, total, most, skew), jnp.int32)
    pairs = (count - 1) // 2
    giver, taker = tallies[1:1 + 2 * pairs:2], tallies[2:2 + 2 * pairs:2]
    room = jnp.minimum(giver - 1, most - taker)
    moved = jax.random.randint(jax.random.fold_in(own_key, 1), (pairs,), 0, 1 << 20) % (room + 1)
    tallies = tallies.at[1:1 + 2 * pairs:2].set(giver - moved).at[2:2 + 2 * pairs:2].set(taker + moved)
    return tallies[jax.random.permutation(jax.random.fold_in(own_key, 2), count)]


def bell_draw(own_key, shape, scale, limit, cuts=(), kind=jnp.bfloat16):
    drawn = scale * jax.random.normal(own_key, shape, jnp.float32)
    if cuts:
        drawn = drawn * block_levels(own_key, shape, cuts, -0.22, 0.18)
    return jnp.clip(drawn, -limit, limit).astype(kind)


def setup_inputs(seed: int = 0, part: int = 0) -> dict:
    key_of = jax.random.split(jax.random.key(seed), 8)
    part_splits = jax.random.split(jax.random.fold_in(key_of[7], part), 8)
    return {
        "latents": bell_draw(part_splits[0], (FRAMES * HL, CLAT, WL), 1.0, 6.0, ((0, 16),)),
        "clip_index": jnp.searchsorted(jnp.cumsum(uneven_parts(part_splits[1], CLIPS, FRAMES, CLIP_MOST, 1)), jnp.arange(FRAMES), side="right").astype(jnp.int32),
        "first_conv": bell_draw(key_of[2], (3, 3, 3, CLAT, CH), (27 * CLAT) ** -0.5, 0.3125),
        "first_gain": jnp.clip(1.0 + 0.12 * jax.random.normal(key_of[3], (CH,), jnp.float32), 0.4, 1.6),
        "middle_conv": bell_draw(key_of[4], (3, 3, 3, CH, CH), (27 * CH) ** -0.5, 0.0625),
        "head_gain": jnp.clip(1.0 + 0.12 * jax.random.normal(key_of[5], (CH,), jnp.float32), 0.4, 1.6),
        "head_weight": bell_draw(key_of[6], (CH, 3 * PATCH), CH ** -0.5, 0.3125),
    }


def causal_conv(field, clip_index, weight):
    frames, height, width, channels = field.shape
    outs = weight.shape[-1]
    ids = jnp.concatenate([jnp.full((2,), -1, jnp.int32), clip_index.astype(jnp.int32)])
    padded = jnp.pad(field, ((2, 0), (1, 1), (1, 1), (0, 0)))
    total = jnp.zeros((frames * height * width, outs), jnp.float32)
    for step_t in range(3):
        keep = (ids[step_t:step_t + frames] == ids[2:]).astype(field.dtype)
        slab = padded[step_t:step_t + frames] * keep[:, None, None, None]
        for step_r in range(3):
            rows = slab[:, step_r:step_r + height]
            stacked = jnp.concatenate([rows[:, :, step_c:step_c + width] for step_c in range(3)], axis=-1)
            stacked = stacked.reshape(-1, 3 * channels)
            total = total + jnp.dot(stacked, weight[step_t, step_r].reshape(3 * channels, outs), preferred_element_type=jnp.float32)
    return total.reshape(frames, height, width, outs)

def norm_act(values, gain):
    scale = lax.rsqrt(lax.optimization_barrier(jnp.mean(values * values, axis=-1, keepdims=True)) + 1e-06)
    return jax.nn.silu(values * scale * gain.astype(jnp.float32))

def reference(latents, clip_index, first_conv, first_gain, middle_conv, head_gain, head_weight):
    video = latents.reshape(FRAMES, HL, CLAT, WL).transpose(0, 1, 3, 2)
    first = causal_conv(video, clip_index, first_conv).astype(jnp.bfloat16)
    active = norm_act(first.astype(jnp.float32), first_gain).astype(jnp.bfloat16)
    summed = first.astype(jnp.float32) + causal_conv(active, clip_index, middle_conv)
    outward = norm_act(summed, head_gain).astype(jnp.bfloat16)
    patch = jnp.dot(outward.reshape(-1, CH), head_weight, preferred_element_type=jnp.float32)
    patch = patch.reshape(FRAMES, HL, WL, 3, PATCH)
    half = PATCH // 2
    front = patch[..., :half]
    back = patch[..., half:]
    moved = jnp.concatenate([jnp.zeros_like(back[:, :, :1]), back[:, :, :-1]], axis=2)
    picture = front + moved
    tiles = picture.reshape(BLOCKS, TF, HL, STRIPS, WS, 3, half)
    tiles = tiles.transpose(0, 3, 1, 5, 2, 4, 6)
    tiles = tiles.reshape(TILES, TF, 3, HL, WS * half)
    return jnp.roll(tiles, STRIPS // 2 - 1, axis=0)
```

```python
import jax
import jax.numpy as jnp
from jax import lax
from jax.experimental import pallas as pl
from jax.experimental.pallas import tpu as pltpu
from jax.sharding import PartitionSpec as P

WS = 16
TF = 2


def norm_act(x, gain):
    scale = lax.rsqrt(jnp.mean(x * x, axis=-1, keepdims=True) + 1e-06)
    v = x * scale * gain
    return v / (1.0 + jnp.exp(-v))


def row_shift(x, by):
    rows = lax.broadcasted_iota(jnp.int32, x.shape, 0)
    n = x.shape[0]
    if by > 0:
        return jnp.where(rows == 0, 0.0, pltpu.roll(x, 1, 0))
    return jnp.where(rows == n - 1, 0.0, pltpu.roll(x, n - 1, 0))


def decode_kernel(
    scal, z_ref, w1_ref, g1_ref, wm_hbm, g2_ref, hw_ref, out_ref,
    wm, act, firstb, fscr, acc, outw, sem,
):
    hl = z_ref.shape[2]
    ch = g1_ref.shape[-1]
    strips = scal[7]
    strip = scal[6]
    patch = hw_ref.shape[-1] // 3
    half = patch // 2
    aw = WS + 3
    ow = WS + 1
    lanes = WS * half

    def tap_copies(dt):
        return [
            pltpu.make_async_copy(
                wm_hbm.at[dt, dr, dc],
                wm.at[dt, pl.ds(dc * ch, ch), pl.ds(dr * ch, ch)],
                sem.at[dt],
            )
            for dr in range(3)
            for dc in range(3)
        ]

    for dt in (2, 1, 0):
        for copy in tap_copies(dt):
            copy.start()

    for f in range(TF + 2):
        if f == 0:
            needed = scal[2] == scal[4]
        elif f == 1:
            needed = jnp.logical_or(scal[3] == scal[4], scal[3] == scal[5])
        else:
            needed = scal[4] == scal[4]

        @pl.when(needed)
        def _(f=f):
            total = None
            for dt in range(3):
                keep = (scal[f + dt] == scal[f + 2]).astype(jnp.float32)
                lhs = z_ref[f + dt].reshape(aw * hl, z_ref.shape[-1])
                if dt < 2:
                    lhs = lhs * keep.astype(jnp.bfloat16)
                part = jnp.dot(lhs, w1_ref[dt], preferred_element_type=jnp.float32)
                total = part if total is None else total + part
            fscr[...] = total.reshape(aw, hl, ch)

            @pl.loop(0, aw)
            def _(w):
                rounded = fscr[w].astype(jnp.bfloat16)
                if f >= 2:
                    firstb[f - 2, w] = rounded
                value = norm_act(rounded.astype(jnp.float32), g1_ref[...])
                col = strip * WS + w - 2
                inside = jnp.logical_and(col >= 0, col < strips * WS).astype(jnp.float32)
                act[f, w] = (value * inside).astype(jnp.bfloat16)

    for dt in (2, 1, 0):
        for copy in tap_copies(dt):
            copy.wait()

        @pl.loop(0, TF)
        def _(fo, dt=dt):
            def unit():
                lhs = jnp.concatenate(
                    [act[fo + dt, pl.ds(dc, ow)].reshape(ow * hl, ch) for dc in range(3)], axis=-1
                )
                return jnp.dot(lhs, wm[dt], preferred_element_type=jnp.float32)

            if dt == 2:
                acc[fo] = unit()
            else:

                @pl.when(scal[fo + dt + 2] == scal[fo + 4])
                def _():
                    acc[fo] += unit()

    rows = lax.broadcasted_iota(jnp.int32, (3 * patch, 6 * lanes), 0)
    cols = lax.broadcasted_iota(jnp.int32, (3 * patch, 6 * lanes), 1)
    odd = cols // (3 * lanes)
    colour = (cols // lanes) % 3
    want = colour * patch + (cols % lanes + half * odd) % patch
    spread = (rows == want).astype(jnp.bfloat16)
    head = jnp.dot(hw_ref[...], spread, preferred_element_type=jnp.float32).astype(jnp.bfloat16)
    lane = lax.broadcasted_iota(jnp.int32, (hl, lanes), 1)

    for fo in range(TF):

        @pl.loop(0, ow)
        def _(w, fo=fo):
            start = pl.multiple_of(w * hl, hl)
            part = acc[fo, pl.ds(start, hl)]
            summed = (
                firstb[fo, w + 1].astype(jnp.float32)
                + row_shift(part[:, :ch], 1)
                + part[:, ch : 2 * ch]
                + row_shift(part[:, 2 * ch :], -1)
            )
            value = norm_act(summed, g2_ref[...])
            inside = jnp.logical_or(strip > 0, w > 0).astype(jnp.float32)
            outw[fo, w % 2, w // 2] = (value * inside).astype(jnp.bfloat16)

        p_odd = jnp.dot(
            outw[fo, 0].reshape(-1, ch), head[:, 3 * lanes :], preferred_element_type=jnp.float32
        )
        p_even = jnp.dot(
            outw[fo, 1, : WS // 2].reshape(-1, ch), head[:, : 3 * lanes],
            preferred_element_type=jnp.float32,
        )
        for k in range(3):
            front = jnp.zeros((hl, lanes), jnp.float32)
            back = jnp.zeros((hl, lanes), jnp.float32)
            for i in range(WS // 2):
                piece = p_even[i * hl : (i + 1) * hl, k * lanes : (k + 1) * lanes]
                front = jnp.where(lane // patch == i, piece, front)
            for i in range(WS // 2 + 1):
                piece = p_odd[i * hl : (i + 1) * hl, k * lanes : (k + 1) * lanes]
                back = jnp.where((lane + half) // patch == i, piece, back)
            out_ref[fo, k] = front + back


def per_device(latents, clip_index, first_conv, first_gain, middle_conv, head_gain, head_weight):
    place = lax.axis_index("tile")
    tiles = lax.axis_size("tile")
    shard_rows, clat, wl = latents.shape
    ch = first_gain.shape[0]
    frames = clip_index.shape[0]
    hl = tiles * shard_rows // frames
    strips = wl // WS
    half = head_weight.shape[1] // 6
    offset = strips // 2 - 1
    rotated = (place - offset) % tiles
    strip = rotated % strips
    block = rotated // strips

    full = lax.all_gather(latents, "tile", axis=0, tiled=True)
    full = full.reshape(frames, hl, clat, wl)
    full = jnp.pad(full, ((4, 0), (0, 0), (0, 0), (3, WS + 5)))
    aw = WS + 3
    win = lax.dynamic_slice(
        full, (block * TF, 0, 0, strip * WS), (TF + 4, hl, clat, WS + 5)
    ).transpose(0, 3, 1, 2)
    win = jnp.pad(win, ((0, 0), (0, 0), (1, 1), (0, 0)))
    z = jnp.concatenate(
        [win[:, dc : dc + aw, dr : dr + hl] for dr in range(3) for dc in range(3)], axis=-1
    )
    ids = jnp.concatenate([jnp.full((4,), -1, jnp.int32), clip_index])
    ids = lax.dynamic_slice_in_dim(ids, block * TF, TF + 4)
    scal = jnp.concatenate([ids, jnp.stack([strip, jnp.int32(strips)]).astype(jnp.int32)])
    vm = pl.BlockSpec(memory_space=pltpu.VMEM)
    out = pl.pallas_call(
        decode_kernel,
        out_shape=jax.ShapeDtypeStruct((TF, 3, hl, WS * half), jnp.float32),
        in_specs=[
            pl.BlockSpec(memory_space=pltpu.SMEM), vm, vm, vm,
            pl.BlockSpec(memory_space=pl.ANY), vm, vm,
        ],
        out_specs=vm,
        scratch_shapes=[
            pltpu.VMEM((3, 3 * ch, 3 * ch), jnp.bfloat16),
            pltpu.VMEM((TF + 2, aw, hl, ch), jnp.bfloat16),
            pltpu.VMEM((TF, aw, hl, ch), jnp.bfloat16),
            pltpu.VMEM((aw, hl, ch), jnp.float32),
            pltpu.VMEM((TF, (WS + 1) * hl, 3 * ch), jnp.float32),
            pltpu.VMEM((TF, 2, WS // 2 + 1, hl, ch), jnp.bfloat16),
            pltpu.SemaphoreType.DMA((3,)),
        ],
        compiler_params=pltpu.CompilerParams(vmem_limit_bytes=60 * 1024 * 1024),
    )(
        scal, z, first_conv.reshape(3, 9 * clat, ch), first_gain.reshape(1, ch), middle_conv,
        head_gain.reshape(1, ch), head_weight,
    )
    return out[None]


def solution(mesh):
    placed = (P(("group", "tile"), None, None), P("group"), P(), P(), P(), P(), P())
    return jax.shard_map(
        per_device,
        mesh=mesh,
        in_specs=placed,
        out_specs=P(("group", "tile"), None, None, None, None),
        check_vma=False,
    )
```

```python
import functools

import jax
import jax.numpy as jnp
from jax import lax
from jax.experimental import pallas as pl
from jax.experimental.pallas import tpu as pltpu
from jax.sharding import PartitionSpec as P

WS = 16
TF = 2
LANES = 128
GAP = LANES // 2


def norm_act(x, gain):
    scale = lax.rsqrt(jnp.mean(x * x, axis=-1, keepdims=True) + 1e-06)
    v = x * scale * gain
    return v / (1.0 + jnp.exp(-v))


def row_shift(x, by):
    rows = lax.broadcasted_iota(jnp.int32, x.shape, 0)
    n = x.shape[0]
    if by > 0:
        return jnp.where(rows == 0, 0.0, pltpu.roll(x, 1, 0))
    return jnp.where(rows == n - 1, 0.0, pltpu.roll(x, n - 1, 0))


def exchange_kernel(sizes, lat_ref, got, pad_a, pad_b, stage, send_sem, recv_sem, own_sem):
    tiles, strips, frames, shard_rows = sizes
    quarters = tiles // frames
    blocks = tiles // strips
    offset = strips // 2 - 1
    me = lax.axis_index("tile")
    barrier = pltpu.get_barrier_semaphore()
    for step in range(1, tiles):
        pl.semaphore_signal(barrier, inc=1, device_id={"tile": lax.rem(me + step, tiles)})

    wl = lat_ref.shape[1]
    values = lat_ref[...].astype(jnp.float32)
    spare = jnp.zeros((2 * LANES - values.shape[0], wl), jnp.float32)
    for pad, rows in ((pad_a, values[:LANES]), (pad_b, jnp.concatenate([values[LANES:], spare]))):
        pad[:8] = jnp.zeros((8, LANES), jnp.float32)
        pad[8 + wl :] = jnp.zeros((WS, LANES), jnp.float32)
        pad[8 : 8 + wl] = rows.T
    low = lax.broadcasted_iota(jnp.int32, (WS, LANES), 1) < LANES // 2
    for s in range(strips):
        stage[s, : 2 * WS] = pad_a[WS * s : WS * (s + 2)].astype(jnp.bfloat16)
        upper = pltpu.roll(pad_b[WS * (s + 1) : WS * (s + 2)], LANES // 2, 1)
        mixed = jnp.where(low, pad_b[WS * s : WS * (s + 1)], upper)
        stage[s, 2 * WS :] = mixed.astype(jnp.bfloat16)
    pl.semaphore_wait(barrier, tiles - 1)

    frame = me // quarters
    quarter = me % quarters

    def each_send(act):
        for ahead in range(3):
            block = frame // TF + ahead
            slot = (2 * TF - TF * ahead + frame % TF) * quarters + quarter

            @pl.when(block < blocks)
            def _():
                @pl.loop(0, strips)
                def _(j):
                    s = (j + me) % strips
                    to = (block * strips + s + offset) % tiles

                    @pl.when(to != me)
                    def _():
                        act(
                            pltpu.make_async_remote_copy(
                                src_ref=stage.at[s],
                                dst_ref=got.at[slot],
                                send_sem=send_sem.at[ahead * strips + s],
                                recv_sem=recv_sem.at[slot],
                                device_id={"tile": to},
                            ),
                            None,
                        )

                    @pl.when(to == me)
                    def _():
                        act(None, pltpu.make_async_copy(stage.at[s], got.at[slot], own_sem))

    def start(remote, local):
        (remote if local is None else local).start()

    def finish(remote, local):
        if local is None:
            remote.wait_send()
        else:
            local.wait()

    each_send(start)
    mine = (me + tiles - offset) % tiles // strips

    @pl.loop(0, 3 * TF * quarters)
    def _(slot):
        source = (TF * mine - 2 * TF) * quarters + slot

        @pl.when(jnp.logical_and(source >= 0, source != me))
        def _():
            pltpu.make_async_remote_copy(
                src_ref=stage.at[0],
                dst_ref=got.at[slot],
                send_sem=send_sem.at[0],
                recv_sem=recv_sem.at[slot],
                device_id={"tile": me},
            ).wait_recv()

    each_send(finish)


def decode_kernel(
    sizes, clip, got_ref, w1_ref, g1_ref, wm_hbm, g2_ref, hw_ref, out_ref,
    wm, act, firstb, fscr, acc, outw, w1, rowtap, z_ref, sem,
):
    tiles, strips, hl, clat, shard_rows = sizes
    ch = g1_ref.shape[-1]
    patch = hw_ref.shape[0] // 3
    half = patch // 2
    aw = WS + 3
    ow = WS + 1
    lanes = WS * half
    rotated = (lax.axis_index("tile") + tiles - (strips // 2 - 1)) % tiles
    strip = rotated % strips
    block = rotated // strips
    scal = []
    for i in range(3 * TF):
        at = block * TF - 2 * TF + i
        scal.append(jnp.where(at < 0, -1, clip[jnp.maximum(at, 0)]))
    g1 = g1_ref[...].reshape(1, ch)
    g2 = g2_ref[...].reshape(1, ch)

    def tap_copies(dt):
        return [
            pltpu.make_async_copy(
                wm_hbm.at[dt, dr, dc],
                wm.at[dt, pl.ds(dc * ch, ch), pl.ds(dr * ch, ch)],
                sem.at[dt],
            )
            for dr in range(3)
            for dc in range(3)
        ]

    for dt in (2, 1, 0):
        for copy in tap_copies(dt):
            copy.start()

    group = 3 * clat
    w1[...] = jnp.zeros_like(w1)
    for dt in range(3):
        for dr in range(3):
            w1[dt, dr * GAP : dr * GAP + group] = w1_ref[dt, dr * group : (dr + 1) * group]
    wide = rowtap.shape[0] // (hl + 2)
    rowtap[:wide] = jnp.zeros((wide, LANES), jnp.float32)
    rowtap[(hl + 1) * wide :] = jnp.zeros((wide, LANES), jnp.float32)
    at_lane = lax.broadcasted_iota(jnp.int32, (wide, LANES), 1)
    quarters = hl // shard_rows
    per = LANES // clat

    for f in range(3 * TF):

        @pl.when(block * TF - 2 * TF + f < 0)
        def _(f=f):
            z_ref[f] = jnp.zeros(z_ref.shape[1:], jnp.bfloat16)

        @pl.when(block * TF - 2 * TF + f >= 0)
        def _(f=f):
            @pl.loop(0, quarters)
            def _(q):
                piece = got_ref[f * quarters + q].astype(jnp.float32)
                tail = piece[2 * WS :]
                tail = jnp.concatenate([tail, pltpu.roll(tail, LANES // 2, 1)])
                for first_row, count, x in ((0, per, piece[: 2 * WS]), (per, shard_rows - per, tail)):
                    shifts = [x[:wide]] + [
                        pltpu.roll(x, 2 * WS - dc, 0)[:wide] for dc in (1, 2)
                    ]
                    for r in range(count):
                        y = jnp.zeros((wide, LANES), jnp.float32)
                        for dc in (2, 1, 0):
                            turn = (dc - r) * clat % LANES
                            moved = pltpu.roll(shifts[dc], turn, 1) if turn else shifts[dc]
                            y = jnp.where(at_lane < (dc + 1) * clat, moved, y)
                        start = (1 + q * shard_rows + first_row + r) * wide
                        rowtap[pl.ds(pl.multiple_of(start, 8), wide)] = y

            @pl.loop(0, aw)
            def _(w):
                v = [
                    rowtap[pl.ds(dr * wide + 8 - 3 + w, hl, stride=wide), :] for dr in range(3)
                ]
                low = v[0] + pltpu.roll(v[1], GAP, 1)
                z_ref[f, w, :, :LANES] = low.astype(jnp.bfloat16)
                z_ref[f, w, :, LANES:] = v[2].astype(jnp.bfloat16)

    for f in range(TF + 2):
        if f == 0:
            needed = scal[2] == scal[4]
        elif f == 1:
            needed = jnp.logical_or(scal[3] == scal[4], scal[3] == scal[5])
        else:
            needed = scal[4] == scal[4]

        @pl.when(needed)
        def _(f=f):
            total = None
            for dt in range(3):
                keep = (scal[f + dt] == scal[f + 2]).astype(jnp.float32)
                lhs = z_ref[f + dt].reshape(aw * hl, z_ref.shape[-1])
                if dt < 2:
                    lhs = lhs * keep.astype(jnp.bfloat16)
                part = jnp.dot(lhs, w1[dt], preferred_element_type=jnp.float32)
                total = part if total is None else total + part
            fscr[...] = total.reshape(aw, hl, ch)

            @pl.loop(0, aw)
            def _(w):
                rounded = fscr[w].astype(jnp.bfloat16)
                if f >= 2:
                    firstb[f - 2, w] = rounded
                value = norm_act(rounded.astype(jnp.float32), g1)
                col = strip * WS + w - 2
                inside = jnp.logical_and(col >= 0, col < strips * WS).astype(jnp.float32)
                act[f, w] = (value * inside).astype(jnp.bfloat16)

    for dt in (2, 1, 0):
        for copy in tap_copies(dt):
            copy.wait()

        @pl.loop(0, TF)
        def _(fo, dt=dt):
            def unit():
                lhs = jnp.concatenate(
                    [act[fo + dt, pl.ds(dc, ow)].reshape(ow * hl, ch) for dc in range(3)], axis=-1
                )
                return jnp.dot(lhs, wm[dt], preferred_element_type=jnp.float32)

            if dt == 2:
                acc[fo] = unit()
            else:

                keep = [(scal[at + dt + 2] == scal[at + 4]).astype(jnp.int32) for at in range(TF)]

                @pl.when(jnp.where(fo == 0, keep[0], keep[1]) == 1)
                def _():
                    acc[fo] += unit()

    rows = lax.broadcasted_iota(jnp.int32, (3 * patch, 6 * lanes), 0)
    cols = lax.broadcasted_iota(jnp.int32, (3 * patch, 6 * lanes), 1)
    odd = cols // (3 * lanes)
    colour = (cols // lanes) % 3
    want = colour * patch + (cols % lanes + half * odd) % patch
    spread = (rows == want).astype(jnp.bfloat16)
    head = lax.dot_general(
        hw_ref[...], spread, (((0,), (0,)), ((), ())), preferred_element_type=jnp.float32
    ).astype(jnp.bfloat16)
    lane = lax.broadcasted_iota(jnp.int32, (hl, lanes), 1)

    for fo in range(TF):

        @pl.loop(0, ow)
        def _(w, fo=fo):
            start = pl.multiple_of(w * hl, hl)
            part = acc[fo, pl.ds(start, hl)]
            summed = (
                firstb[fo, w + 1].astype(jnp.float32)
                + row_shift(part[:, :ch], 1)
                + part[:, ch : 2 * ch]
                + row_shift(part[:, 2 * ch :], -1)
            )
            value = norm_act(summed, g2)
            inside = jnp.logical_or(strip > 0, w > 0).astype(jnp.float32)
            outw[fo, w % 2, w // 2] = (value * inside).astype(jnp.bfloat16)

        p_odd = jnp.dot(
            outw[fo, 0].reshape(-1, ch), head[:, 3 * lanes :], preferred_element_type=jnp.float32
        )
        p_even = jnp.dot(
            outw[fo, 1, : WS // 2].reshape(-1, ch), head[:, : 3 * lanes],
            preferred_element_type=jnp.float32,
        )
        for k in range(3):
            front = jnp.zeros((hl, lanes), jnp.float32)
            back = jnp.zeros((hl, lanes), jnp.float32)
            for i in range(WS // 2):
                piece = p_even[i * hl : (i + 1) * hl, k * lanes : (k + 1) * lanes]
                front = jnp.where(lane // patch == i, piece, front)
            for i in range(WS // 2 + 1):
                piece = p_odd[i * hl : (i + 1) * hl, k * lanes : (k + 1) * lanes]
                back = jnp.where((lane + half) // patch == i, piece, back)
            out_ref[fo, k] = front + back


def per_device(latents, clip_index, first_conv, first_gain, middle_conv, head_gain, head_weight):
    tiles = lax.axis_size("tile")
    shard_rows, clat, wl = latents.shape
    ch = first_gain.shape[0]
    frames = clip_index.shape[0]
    hl = tiles * shard_rows // frames
    strips = wl // WS
    half = head_weight.shape[1] // 6
    aw = WS + 3
    quarters = tiles // frames
    slots = 3 * TF * quarters
    got = pl.pallas_call(
        functools.partial(exchange_kernel, (tiles, strips, frames, shard_rows)),
        out_shape=jax.ShapeDtypeStruct((slots, 3 * WS, LANES), jnp.bfloat16),
        in_specs=[pl.BlockSpec(memory_space=pltpu.VMEM)],
        out_specs=pl.BlockSpec(memory_space=pl.ANY),
        scratch_shapes=[
            pltpu.VMEM((8 + wl + WS, LANES), jnp.float32),
            pltpu.VMEM((8 + wl + WS, LANES), jnp.float32),
            pltpu.VMEM((strips, 3 * WS, LANES), jnp.bfloat16),
            pltpu.SemaphoreType.DMA((3 * strips,)),
            pltpu.SemaphoreType.DMA((slots,)),
            pltpu.SemaphoreType.DMA,
        ],
        compiler_params=pltpu.CompilerParams(collective_id=0, has_side_effects=True),
    )(latents.reshape(shard_rows * clat, wl))
    vm = pl.BlockSpec(memory_space=pltpu.VMEM)
    out = pl.pallas_call(
        functools.partial(decode_kernel, (tiles, strips, hl, clat, shard_rows)),
        out_shape=jax.ShapeDtypeStruct((TF, 3, hl, WS * half), jnp.float32),
        in_specs=[
            pl.BlockSpec(memory_space=pltpu.SMEM), vm, vm, vm,
            pl.BlockSpec(memory_space=pl.ANY), vm, vm,
        ],
        out_specs=vm,
        scratch_shapes=[
            pltpu.VMEM((3, 3 * ch, 3 * ch), jnp.bfloat16),
            pltpu.VMEM((TF + 2, aw, hl, ch), jnp.bfloat16),
            pltpu.VMEM((TF, aw, hl, ch), jnp.bfloat16),
            pltpu.VMEM((aw, hl, ch), jnp.float32),
            pltpu.VMEM((TF, (WS + 1) * hl, 3 * ch), jnp.float32),
            pltpu.VMEM((TF, 2, WS // 2 + 1, hl, ch), jnp.bfloat16),
            pltpu.VMEM((3, 2 * LANES, ch), jnp.bfloat16),
            pltpu.VMEM(((hl + 2) * 24, LANES), jnp.float32),
            pltpu.VMEM((3 * TF, aw, hl, 2 * LANES), jnp.bfloat16),
            pltpu.SemaphoreType.DMA((3,)),
        ],
        compiler_params=pltpu.CompilerParams(vmem_limit_bytes=60 * 1024 * 1024),
    )(
        clip_index, got, first_conv.reshape(3, 9 * clat, ch), first_gain, middle_conv,
        head_gain, head_weight.T,
    )
    return out[None]


def solution(mesh):
    placed = (P(("group", "tile"), None, None), P("group"), P(), P(), P(), P(), P())
    return jax.shard_map(
        per_device,
        mesh=mesh,
        in_specs=placed,
        out_specs=P(("group", "tile"), None, None, None, None),
        check_vma=False,
    )
```

```python
import functools

import jax
import jax.numpy as jnp
from jax import lax
from jax.experimental import pallas as pl
from jax.experimental.pallas import tpu as pltpu
from jax.sharding import PartitionSpec as P

WS = 16
TF = 2
LANES = 128
GAP = LANES // 2
WIDE = WS + 5
HALF = (WIDE + 1) // 2


def norm_act(x, gain):
    scale = lax.rsqrt(jnp.mean(x * x, axis=-1, keepdims=True) + 1e-06)
    h = x * scale * (0.5 * gain)
    return h + h * jnp.tanh(h)


def row_shift(x, by):
    rows = lax.broadcasted_iota(jnp.int32, x.shape, 0)
    n = x.shape[0]
    if by > 0:
        return jnp.where(rows == 0, 0.0, pltpu.roll(x, 1, 0))
    return jnp.where(rows == n - 1, 0.0, pltpu.roll(x, n - 1, 0))


def exchange_kernel(sizes, lat_ref, got, pad_a, pad_b, packed, stage, send_sem, recv_sem, own_sem):
    tiles, strips, frames, shard_rows = sizes
    quarters = tiles // frames
    blocks = tiles // strips
    offset = strips // 2 - 1
    me = lax.axis_index("tile")
    barrier = pltpu.get_barrier_semaphore()
    for step in range(1, tiles):
        pl.semaphore_signal(barrier, inc=1, device_id={"tile": lax.rem(me + step, tiles)})

    wl = lat_ref.shape[1]
    values = lat_ref[...].astype(jnp.float32)
    spare = jnp.zeros((2 * LANES - values.shape[0], wl), jnp.float32)
    for pad, rows in ((pad_a, values[:LANES]), (pad_b, jnp.concatenate([values[LANES:], spare]))):
        pad[:8] = jnp.zeros((8, LANES), jnp.float32)
        pad[8 + wl :] = jnp.zeros((WS, LANES), jnp.float32)
        pad[8 : 8 + wl] = rows.T
    low = lax.broadcasted_iota(jnp.int32, (HALF, LANES), 1) < LANES // 2
    for s in range(strips):
        at = WS * s + 8 - 3
        packed[s, :WIDE] = pad_a[at : at + WIDE]
        upper = pltpu.roll(pad_b[at + HALF : at + 2 * HALF], LANES // 2, 1)
        packed[s, WIDE:] = jnp.where(low, pad_b[at : at + HALF], upper)
        stage[s] = packed[s].astype(jnp.bfloat16)
    pl.semaphore_wait(barrier, tiles - 1)

    frame = me // quarters
    quarter = me % quarters

    def each_send(act):
        for ahead in range(3):
            block = frame // TF + ahead
            slot = (2 * TF - TF * ahead + frame % TF) * quarters + quarter

            @pl.when(block < blocks)
            def _():
                @pl.loop(0, strips)
                def _(j):
                    s = (j + me) % strips
                    to = (block * strips + s + offset) % tiles

                    @pl.when(to != me)
                    def _():
                        act(
                            pltpu.make_async_remote_copy(
                                src_ref=stage.at[s],
                                dst_ref=got.at[slot],
                                send_sem=send_sem.at[ahead * strips + s],
                                recv_sem=recv_sem.at[slot],
                                device_id={"tile": to},
                            ),
                            None,
                        )

                    @pl.when(to == me)
                    def _():
                        act(None, pltpu.make_async_copy(stage.at[s], got.at[slot], own_sem))

    def start(remote, local):
        (remote if local is None else local).start()

    def finish(remote, local):
        if local is None:
            remote.wait_send()
        else:
            local.wait()

    each_send(start)
    mine = (me + tiles - offset) % tiles // strips

    @pl.loop(0, 3 * TF * quarters)
    def _(slot):
        source = (TF * mine - 2 * TF) * quarters + slot

        @pl.when(jnp.logical_and(source >= 0, source != me))
        def _():
            pltpu.make_async_remote_copy(
                src_ref=stage.at[0],
                dst_ref=got.at[slot],
                send_sem=send_sem.at[0],
                recv_sem=recv_sem.at[slot],
                device_id={"tile": me},
            ).wait_recv()

    each_send(finish)


def decode_kernel(
    sizes, clip, got_ref, w1_ref, g1_ref, wm_hbm, g2_ref, hw_ref, out_ref,
    wm, act, firstb, fscr, acc, outw, w1, main, tail, rowtap, z_ref, sem,
):
    tiles, strips, hl, clat, shard_rows = sizes
    ch = g1_ref.shape[-1]
    patch = hw_ref.shape[0] // 3
    half = patch // 2
    aw = WS + 3
    ow = WS + 1
    lanes = WS * half
    rotated = (lax.axis_index("tile") + tiles - (strips // 2 - 1)) % tiles
    strip = rotated % strips
    block = rotated // strips
    scal = []
    for i in range(3 * TF):
        at = block * TF - 2 * TF + i
        scal.append(jnp.where(at < 0, -1, clip[jnp.maximum(at, 0)]))
    g1 = g1_ref[...].reshape(1, ch)
    g2 = g2_ref[...].reshape(1, ch)

    def tap_copies(dt):
        return [
            pltpu.make_async_copy(
                wm_hbm.at[dt, dr, dc],
                wm.at[dt, pl.ds(dc * ch, ch), pl.ds(dr * ch, ch)],
                sem.at[dt],
            )
            for dr in range(3)
            for dc in range(3)
        ]

    for dt in (2, 1, 0):
        for copy in tap_copies(dt):
            copy.start()

    group = 3 * clat
    w1[...] = jnp.zeros_like(w1)
    for dt in range(3):
        for dr in range(3):
            w1[dt, dr * GAP : dr * GAP + group] = w1_ref[dt, dr * group : (dr + 1) * group]
    wide = rowtap.shape[0] // (hl + 2)
    rowtap[:wide] = jnp.zeros((wide, LANES), jnp.float32)
    rowtap[(hl + 1) * wide :] = jnp.zeros((wide, LANES), jnp.float32)
    at_lane = lax.broadcasted_iota(jnp.int32, (wide, LANES), 1)
    quarters = hl // shard_rows
    per = LANES // clat

    for f in range(3 * TF):

        @pl.when(block * TF - 2 * TF + f < 0)
        def _(f=f):
            z_ref[f] = jnp.zeros(z_ref.shape[1:], jnp.bfloat16)

        @pl.when(block * TF - 2 * TF + f >= 0)
        def _(f=f):
            @pl.loop(0, quarters)
            def _(q):
                main[...] = got_ref[f * quarters + q].astype(jnp.float32)
                tail[:HALF] = main[WIDE:]
                tail[HALF : 2 * HALF] = pltpu.roll(main[WIDE:], LANES // 2, 1)
                for first_row, count, x in ((0, per, main), (per, shard_rows - per, tail)):
                    shifts = [x[dc : dc + wide] for dc in range(3)]
                    for r in range(count):
                        y = jnp.zeros((wide, LANES), jnp.float32)
                        for dc in (2, 1, 0):
                            turn = (dc - r) * clat % LANES
                            moved = pltpu.roll(shifts[dc], turn, 1) if turn else shifts[dc]
                            y = jnp.where(at_lane < (dc + 1) * clat, moved, y)
                        start = (1 + q * shard_rows + first_row + r) * wide
                        rowtap[pl.ds(pl.multiple_of(start, 8), wide)] = y

            for w in range(aw):
                v = [
                    rowtap[pl.ds(dr * wide + w, hl, stride=wide), :] for dr in range(3)
                ]
                low = v[0] + pltpu.roll(v[1], GAP, 1)
                z_ref[f, w, :, :LANES] = low.astype(jnp.bfloat16)
                z_ref[f, w, :, LANES:] = v[2].astype(jnp.bfloat16)

    for f in range(TF + 2):
        if f == 0:
            needed = scal[2] == scal[4]
        elif f == 1:
            needed = jnp.logical_or(scal[3] == scal[4], scal[3] == scal[5])
        else:
            needed = scal[4] == scal[4]

        @pl.when(needed)
        def _(f=f):
            taps = []
            for dt in range(3):
                keep = (scal[f + dt] == scal[f + 2]).astype(jnp.float32)
                lhs = z_ref[f + dt].reshape(aw * hl, z_ref.shape[-1])
                taps.append(lhs * keep.astype(jnp.bfloat16) if dt < 2 else lhs)
            fscr[...] = jnp.dot(
                jnp.concatenate(taps, axis=-1), w1[...].reshape(-1, ch),
                preferred_element_type=jnp.float32,
            ).reshape(aw, hl, ch)

            for w in range(aw):
                rounded = fscr[w].astype(jnp.bfloat16)
                if f >= 2:
                    firstb[f - 2, w] = rounded
                value = norm_act(rounded.astype(jnp.float32), g1)
                if w < 2:
                    value = value * (strip > 0).astype(jnp.float32)
                if w == aw - 1:
                    value = value * (strip < strips - 1).astype(jnp.float32)
                act[f, w] = value.astype(jnp.bfloat16)

    for dt in (2, 1, 0):
        for copy in tap_copies(dt):
            copy.wait()

        @pl.loop(0, TF)
        def _(fo, dt=dt):
            def unit():
                lhs = jnp.concatenate(
                    [act[fo + dt, pl.ds(dc, ow)].reshape(ow * hl, ch) for dc in range(3)], axis=-1
                )
                return jnp.dot(lhs, wm[dt], preferred_element_type=jnp.float32)

            if dt == 2:
                acc[fo] = unit()
            else:

                keep = [(scal[at + dt + 2] == scal[at + 4]).astype(jnp.int32) for at in range(TF)]

                @pl.when(jnp.where(fo == 0, keep[0], keep[1]) == 1)
                def _():
                    acc[fo] += unit()

    rows = lax.broadcasted_iota(jnp.int32, (3 * patch, 6 * lanes), 0)
    cols = lax.broadcasted_iota(jnp.int32, (3 * patch, 6 * lanes), 1)
    odd = cols // (3 * lanes)
    colour = (cols // lanes) % 3
    want = colour * patch + (cols % lanes + half * odd) % patch
    spread = (rows == want).astype(jnp.bfloat16)
    head = lax.dot_general(
        hw_ref[...], spread, (((0,), (0,)), ((), ())), preferred_element_type=jnp.float32
    ).astype(jnp.bfloat16)
    lane = lax.broadcasted_iota(jnp.int32, (hl, lanes), 1)

    for fo in range(TF):
        for w in range(ow):
            part = acc[fo, w * hl : (w + 1) * hl]
            summed = (
                firstb[fo, w + 1].astype(jnp.float32)
                + row_shift(part[:, :ch], 1)
                + part[:, ch : 2 * ch]
                + row_shift(part[:, 2 * ch :], -1)
            )
            value = norm_act(summed, g2)
            if w == 0:
                value = value * (strip > 0).astype(jnp.float32)
            outw[fo, w % 2, w // 2] = value.astype(jnp.bfloat16)

        p_odd = jnp.dot(
            outw[fo, 0].reshape(-1, ch), head[:, 3 * lanes :], preferred_element_type=jnp.float32
        )
        p_even = jnp.dot(
            outw[fo, 1, : WS // 2].reshape(-1, ch), head[:, : 3 * lanes],
            preferred_element_type=jnp.float32,
        )
        for k in range(3):
            front = jnp.zeros((hl, lanes), jnp.float32)
            back = jnp.zeros((hl, lanes), jnp.float32)
            for i in range(WS // 2):
                piece = p_even[i * hl : (i + 1) * hl, k * lanes : (k + 1) * lanes]
                front = jnp.where(lane // patch == i, piece, front)
            for i in range(WS // 2 + 1):
                piece = p_odd[i * hl : (i + 1) * hl, k * lanes : (k + 1) * lanes]
                back = jnp.where((lane + half) // patch == i, piece, back)
            out_ref[fo, k] = front + back


def per_device(latents, clip_index, first_conv, first_gain, middle_conv, head_gain, head_weight):
    tiles = lax.axis_size("tile")
    shard_rows, clat, wl = latents.shape
    ch = first_gain.shape[0]
    frames = clip_index.shape[0]
    hl = tiles * shard_rows // frames
    strips = wl // WS
    half = head_weight.shape[1] // 6
    aw = WS + 3
    quarters = tiles // frames
    slots = 3 * TF * quarters
    got = pl.pallas_call(
        functools.partial(exchange_kernel, (tiles, strips, frames, shard_rows)),
        out_shape=jax.ShapeDtypeStruct((slots, WIDE + HALF, LANES), jnp.bfloat16),
        in_specs=[pl.BlockSpec(memory_space=pltpu.VMEM)],
        out_specs=pl.BlockSpec(memory_space=pl.ANY),
        scratch_shapes=[
            pltpu.VMEM((8 + wl + WS, LANES), jnp.float32),
            pltpu.VMEM((8 + wl + WS, LANES), jnp.float32),
            pltpu.VMEM((strips, WIDE + HALF, LANES), jnp.float32),
            pltpu.VMEM((strips, WIDE + HALF, LANES), jnp.bfloat16),
            pltpu.SemaphoreType.DMA((3 * strips,)),
            pltpu.SemaphoreType.DMA((slots,)),
            pltpu.SemaphoreType.DMA,
        ],
        compiler_params=pltpu.CompilerParams(collective_id=0, has_side_effects=True),
    )(latents.reshape(shard_rows * clat, wl))
    vm = pl.BlockSpec(memory_space=pltpu.VMEM)
    out = pl.pallas_call(
        functools.partial(decode_kernel, (tiles, strips, hl, clat, shard_rows)),
        out_shape=jax.ShapeDtypeStruct((TF, 3, hl, WS * half), jnp.float32),
        in_specs=[
            pl.BlockSpec(memory_space=pltpu.SMEM), vm, vm, vm,
            pl.BlockSpec(memory_space=pl.ANY), vm, vm,
        ],
        out_specs=vm,
        scratch_shapes=[
            pltpu.VMEM((3, 3 * ch, 3 * ch), jnp.bfloat16),
            pltpu.VMEM((TF + 2, aw, hl, ch), jnp.bfloat16),
            pltpu.VMEM((TF, aw, hl, ch), jnp.bfloat16),
            pltpu.VMEM((aw, hl, ch), jnp.float32),
            pltpu.VMEM((TF, (WS + 1) * hl, 3 * ch), jnp.float32),
            pltpu.VMEM((TF, 2, WS // 2 + 1, hl, ch), jnp.bfloat16),
            pltpu.VMEM((3, 2 * LANES, ch), jnp.bfloat16),
            pltpu.VMEM((WIDE + HALF, LANES), jnp.float32),
            pltpu.VMEM((WIDE + HALF, LANES), jnp.float32),
            pltpu.VMEM(((hl + 2) * 24, LANES), jnp.float32),
            pltpu.VMEM((3 * TF, aw, hl, 2 * LANES), jnp.bfloat16),
            pltpu.SemaphoreType.DMA((3,)),
        ],
        compiler_params=pltpu.CompilerParams(vmem_limit_bytes=60 * 1024 * 1024),
    )(
        clip_index, got, first_conv.reshape(3, 9 * clat, ch), first_gain, middle_conv,
        head_gain, head_weight.T,
    )
    return out[None]


def solution(mesh):
    placed = (P(("group", "tile"), None, None), P("group"), P(), P(), P(), P(), P())
    return jax.shard_map(
        per_device,
        mesh=mesh,
        in_specs=placed,
        out_specs=P(("group", "tile"), None, None, None, None),
        check_vma=False,
    )
```

```python
import functools

import jax
import jax.numpy as jnp
from jax import lax
from jax.experimental import pallas as pl
from jax.experimental.pallas import tpu as pltpu
from jax.sharding import PartitionSpec as P

WS = 16
TF = 2
LANES = 128
GAP = LANES // 2
WIDE = WS + 5
HALF = (WIDE + 1) // 2


def norm_act(x, gain):
    scale = lax.rsqrt(jnp.mean(x * x, axis=-1, keepdims=True) + 1e-06)
    h = x * scale * (0.5 * gain)
    return h + h * jnp.tanh(h)


def row_shift(x, by):
    rows = lax.broadcasted_iota(jnp.int32, x.shape, 0)
    n = x.shape[0]
    if by > 0:
        return jnp.where(rows == 0, 0.0, pltpu.roll(x, 1, 0))
    return jnp.where(rows == n - 1, 0.0, pltpu.roll(x, n - 1, 0))


def exchange_kernel(sizes, lat_ref, got, pad_a, pad_b, packed, stage, send_sem, recv_sem, own_sem):
    tiles, strips, frames, shard_rows = sizes
    quarters = tiles // frames
    blocks = tiles // strips
    offset = strips // 2 - 1
    me = lax.axis_index("tile")
    barrier = pltpu.get_barrier_semaphore()
    for step in range(1, tiles):
        pl.semaphore_signal(barrier, inc=1, device_id={"tile": lax.rem(me + step, tiles)})

    wl = lat_ref.shape[1]
    values = lat_ref[...].astype(jnp.float32)
    spare = jnp.zeros((2 * LANES - values.shape[0], wl), jnp.float32)
    for pad, rows in ((pad_a, values[:LANES]), (pad_b, jnp.concatenate([values[LANES:], spare]))):
        pad[:8] = jnp.zeros((8, LANES), jnp.float32)
        pad[8 + wl :] = jnp.zeros((WS, LANES), jnp.float32)
        pad[8 : 8 + wl] = rows.T
    low = lax.broadcasted_iota(jnp.int32, (HALF, LANES), 1) < LANES // 2
    for s in range(strips):
        at = WS * s + 8 - 3
        packed[s, :WIDE] = pad_a[at : at + WIDE]
        upper = pltpu.roll(pad_b[at + HALF : at + 2 * HALF], LANES // 2, 1)
        packed[s, WIDE:] = jnp.where(low, pad_b[at : at + HALF], upper)
        stage[s] = packed[s].astype(jnp.bfloat16)
    pl.semaphore_wait(barrier, tiles - 1)

    frame = me // quarters
    quarter = me % quarters

    def each_send(act):
        for ahead in range(3):
            block = frame // TF + ahead
            slot = (2 * TF - TF * ahead + frame % TF) * quarters + quarter

            @pl.when(block < blocks)
            def _():
                @pl.loop(0, strips)
                def _(j):
                    s = (j + me) % strips
                    to = (block * strips + s + offset) % tiles

                    @pl.when(to != me)
                    def _():
                        act(
                            pltpu.make_async_remote_copy(
                                src_ref=stage.at[s],
                                dst_ref=got.at[slot],
                                send_sem=send_sem.at[ahead * strips + s],
                                recv_sem=recv_sem.at[slot],
                                device_id={"tile": to},
                            ),
                            None,
                        )

                    @pl.when(to == me)
                    def _():
                        act(None, pltpu.make_async_copy(stage.at[s], got.at[slot], own_sem))

    def start(remote, local):
        (remote if local is None else local).start()

    def finish(remote, local):
        if local is None:
            remote.wait_send()
        else:
            local.wait()

    each_send(start)
    mine = (me + tiles - offset) % tiles // strips

    @pl.loop(0, 3 * TF * quarters)
    def _(slot):
        source = (TF * mine - 2 * TF) * quarters + slot

        @pl.when(jnp.logical_and(source >= 0, source != me))
        def _():
            pltpu.make_async_remote_copy(
                src_ref=stage.at[0],
                dst_ref=got.at[slot],
                send_sem=send_sem.at[0],
                recv_sem=recv_sem.at[slot],
                device_id={"tile": me},
            ).wait_recv()

    each_send(finish)


def decode_kernel(
    sizes, clip, got_ref, w1_ref, g1_ref, wm_hbm, g2_ref, hw_ref, out_ref,
    wm, act, firstb, fscr, acc, outw, w1, main, tail, rowtap, z_ref, sem,
):
    tiles, strips, hl, clat, shard_rows = sizes
    ch = g1_ref.shape[-1]
    patch = hw_ref.shape[0] // 3
    half = patch // 2
    aw = WS + 3
    ow = WS + 1
    lanes = WS * half
    rotated = (lax.axis_index("tile") + tiles - (strips // 2 - 1)) % tiles
    strip = rotated % strips
    block = rotated // strips
    scal = []
    for i in range(3 * TF):
        at = block * TF - 2 * TF + i
        scal.append(jnp.where(at < 0, -1, clip[jnp.maximum(at, 0)]))
    g1 = g1_ref[...].reshape(1, ch)
    g2 = g2_ref[...].reshape(1, ch)

    def tap_copies(dt):
        return [
            pltpu.make_async_copy(
                wm_hbm.at[dt, dr, dc],
                wm.at[pl.ds(dc * ch, ch), pl.ds((3 * dt + dr) * ch, ch)],
                sem.at[dt],
            )
            for dr in range(3)
            for dc in range(3)
        ]

    for dt in (2, 1, 0):
        for copy in tap_copies(dt):
            copy.start()

    group = 3 * clat
    w1[...] = jnp.zeros_like(w1)
    for dt in range(3):
        for dr in range(3):
            w1[dt, dr * GAP : dr * GAP + group] = w1_ref[dt, dr * group : (dr + 1) * group]
    wide = rowtap.shape[0] // (hl + 2)
    rowtap[:wide] = jnp.zeros((wide, LANES), jnp.float32)
    rowtap[(hl + 1) * wide :] = jnp.zeros((wide, LANES), jnp.float32)
    at_lane = lax.broadcasted_iota(jnp.int32, (wide, LANES), 1)
    quarters = hl // shard_rows
    per = LANES // clat

    for f in range(3 * TF):

        @pl.when(block * TF - 2 * TF + f < 0)
        def _(f=f):
            z_ref[f] = jnp.zeros(z_ref.shape[1:], jnp.bfloat16)

        @pl.when(block * TF - 2 * TF + f >= 0)
        def _(f=f):
            for q in range(quarters):
                main[q] = got_ref[f * quarters + q].astype(jnp.float32)
                tail[q, :HALF] = main[q, WIDE:]
                tail[q, HALF : 2 * HALF] = pltpu.roll(main[q, WIDE:], LANES // 2, 1)
                for first_row, count, x in ((0, per, main.at[q]), (per, shard_rows - per, tail.at[q])):
                    shifts = [x[dc : dc + wide] for dc in range(3)]
                    for r in range(count):
                        y = jnp.zeros((wide, LANES), jnp.float32)
                        for dc in (2, 1, 0):
                            turn = (dc - r) * clat % LANES
                            moved = pltpu.roll(shifts[dc], turn, 1) if turn else shifts[dc]
                            y = jnp.where(at_lane < (dc + 1) * clat, moved, y)
                        start = (1 + q * shard_rows + first_row + r) * wide
                        rowtap[start : start + wide] = y

            for w in range(aw):
                v = [
                    rowtap[pl.ds(dr * wide + w, hl, stride=wide), :] for dr in range(3)
                ]
                low = v[0] + pltpu.roll(v[1], GAP, 1)
                z_ref[f, w, :, :LANES] = low.astype(jnp.bfloat16)
                z_ref[f, w, :, LANES:] = v[2].astype(jnp.bfloat16)

    for f in range(TF + 2):
        if f == 0:
            needed = scal[2] == scal[4]
        elif f == 1:
            needed = jnp.logical_or(scal[3] == scal[4], scal[3] == scal[5])
        else:
            needed = scal[4] == scal[4]

        @pl.when(needed)
        def _(f=f):
            taps = []
            for dt in range(3):
                keep = (scal[f + dt] == scal[f + 2]).astype(jnp.float32)
                lhs = z_ref[f + dt].reshape(aw * hl, z_ref.shape[-1])
                taps.append(lhs * keep.astype(jnp.bfloat16) if dt < 2 else lhs)
            fscr[...] = jnp.dot(
                jnp.concatenate(taps, axis=-1), w1[...].reshape(-1, ch),
                preferred_element_type=jnp.float32,
            ).reshape(aw, hl, ch)

            for w in range(aw):
                rounded = fscr[w].astype(jnp.bfloat16)
                if f >= 2:
                    firstb[f - 2, w] = rounded
                value = norm_act(rounded.astype(jnp.float32), g1)
                if w < 2:
                    value = value * (strip > 0).astype(jnp.float32)
                if w == aw - 1:
                    value = value * (strip < strips - 1).astype(jnp.float32)
                act[f, w] = value.astype(jnp.bfloat16)

    wide_out = 3 * ch

    def unit(f, start, count):
        lhs = jnp.concatenate(
            [act[f, pl.ds(dc, ow)].reshape(ow * hl, ch) for dc in range(3)], axis=-1
        )
        taps = wm[:, start * wide_out : (start + count) * wide_out]
        return jnp.dot(lhs, taps, preferred_element_type=jnp.float32)

    def arrived(dt):
        for copy in tap_copies(dt):
            copy.wait()

    arrived(2)
    acc[:, :wide_out] = unit(3, 2, 1)
    arrived(1)

    @pl.when(scal[4] == scal[5])
    def _():
        both = unit(2, 1, 2)
        acc[:, :wide_out] += both[:, :wide_out]
        acc[:, wide_out:] = both[:, wide_out:]

    @pl.when(scal[4] != scal[5])
    def _():
        acc[:, wide_out:] = unit(2, 2, 1)

    arrived(0)

    @pl.when(scal[3] == scal[5])
    def _():
        acc[...] += unit(1, 0, 2)

    @pl.when(jnp.logical_and(scal[3] == scal[4], scal[3] != scal[5]))
    def _():
        acc[:, wide_out:] += unit(1, 1, 1)

    @pl.when(scal[2] == scal[4])
    def _():
        acc[:, wide_out:] += unit(0, 0, 1)

    rows = lax.broadcasted_iota(jnp.int32, (3 * patch, 6 * lanes), 0)
    cols = lax.broadcasted_iota(jnp.int32, (3 * patch, 6 * lanes), 1)
    odd = cols // (3 * lanes)
    colour = (cols // lanes) % 3
    want = colour * patch + (cols % lanes + half * odd) % patch
    spread = (rows == want).astype(jnp.bfloat16)
    head = lax.dot_general(
        hw_ref[...], spread, (((0,), (0,)), ((), ())), preferred_element_type=jnp.float32
    ).astype(jnp.bfloat16)
    lane = lax.broadcasted_iota(jnp.int32, (hl, lanes), 1)

    for fo in range(TF):
        for w in range(ow):
            part = acc[w * hl : (w + 1) * hl, (1 - fo) * wide_out : (2 - fo) * wide_out]
            summed = (
                firstb[fo, w + 1].astype(jnp.float32)
                + row_shift(part[:, :ch], 1)
                + part[:, ch : 2 * ch]
                + row_shift(part[:, 2 * ch :], -1)
            )
            value = norm_act(summed, g2)
            if w == 0:
                value = value * (strip > 0).astype(jnp.float32)
            outw[fo, w % 2, w // 2] = value.astype(jnp.bfloat16)

        p_odd = jnp.dot(
            outw[fo, 0].reshape(-1, ch), head[:, 3 * lanes :], preferred_element_type=jnp.float32
        )
        p_even = jnp.dot(
            outw[fo, 1, : WS // 2].reshape(-1, ch), head[:, : 3 * lanes],
            preferred_element_type=jnp.float32,
        )
        for k in range(3):
            front = jnp.zeros((hl, lanes), jnp.float32)
            back = jnp.zeros((hl, lanes), jnp.float32)
            for i in range(WS // 2):
                piece = p_even[i * hl : (i + 1) * hl, k * lanes : (k + 1) * lanes]
                front = jnp.where(lane // patch == i, piece, front)
            for i in range(WS // 2 + 1):
                piece = p_odd[i * hl : (i + 1) * hl, k * lanes : (k + 1) * lanes]
                back = jnp.where((lane + half) // patch == i, piece, back)
            out_ref[fo, k] = front + back


def per_device(latents, clip_index, first_conv, first_gain, middle_conv, head_gain, head_weight):
    tiles = lax.axis_size("tile")
    shard_rows, clat, wl = latents.shape
    ch = first_gain.shape[0]
    frames = clip_index.shape[0]
    hl = tiles * shard_rows // frames
    strips = wl // WS
    half = head_weight.shape[1] // 6
    aw = WS + 3
    quarters = tiles // frames
    slots = 3 * TF * quarters
    got = pl.pallas_call(
        functools.partial(exchange_kernel, (tiles, strips, frames, shard_rows)),
        out_shape=jax.ShapeDtypeStruct((slots, WIDE + HALF, LANES), jnp.bfloat16),
        in_specs=[pl.BlockSpec(memory_space=pltpu.VMEM)],
        out_specs=pl.BlockSpec(memory_space=pl.ANY),
        scratch_shapes=[
            pltpu.VMEM((8 + wl + WS, LANES), jnp.float32),
            pltpu.VMEM((8 + wl + WS, LANES), jnp.float32),
            pltpu.VMEM((strips, WIDE + HALF, LANES), jnp.float32),
            pltpu.VMEM((strips, WIDE + HALF, LANES), jnp.bfloat16),
            pltpu.SemaphoreType.DMA((3 * strips,)),
            pltpu.SemaphoreType.DMA((slots,)),
            pltpu.SemaphoreType.DMA,
        ],
        compiler_params=pltpu.CompilerParams(collective_id=0, has_side_effects=True),
    )(latents.reshape(shard_rows * clat, wl))
    vm = pl.BlockSpec(memory_space=pltpu.VMEM)
    out = pl.pallas_call(
        functools.partial(decode_kernel, (tiles, strips, hl, clat, shard_rows)),
        out_shape=jax.ShapeDtypeStruct((TF, 3, hl, WS * half), jnp.float32),
        in_specs=[
            pl.BlockSpec(memory_space=pltpu.SMEM), vm, vm, vm,
            pl.BlockSpec(memory_space=pl.ANY), vm, vm,
        ],
        out_specs=vm,
        scratch_shapes=[
            pltpu.VMEM((3 * ch, 9 * ch), jnp.bfloat16),
            pltpu.VMEM((TF + 2, aw, hl, ch), jnp.bfloat16),
            pltpu.VMEM((TF, aw, hl, ch), jnp.bfloat16),
            pltpu.VMEM((aw, hl, ch), jnp.float32),
            pltpu.VMEM(((WS + 1) * hl, TF * 3 * ch), jnp.float32),
            pltpu.VMEM((TF, 2, WS // 2 + 1, hl, ch), jnp.bfloat16),
            pltpu.VMEM((3, 2 * LANES, ch), jnp.bfloat16),
            pltpu.VMEM((quarters, WIDE + HALF, LANES), jnp.float32),
            pltpu.VMEM((quarters, WIDE + HALF, LANES), jnp.float32),
            pltpu.VMEM(((hl + 2) * 24, LANES), jnp.float32),
            pltpu.VMEM((3 * TF, aw, hl, 2 * LANES), jnp.bfloat16),
            pltpu.SemaphoreType.DMA((3,)),
        ],
        compiler_params=pltpu.CompilerParams(vmem_limit_bytes=60 * 1024 * 1024),
    )(
        clip_index, got, first_conv.reshape(3, 9 * clat, ch), first_gain, middle_conv,
        head_gain, head_weight.T,
    )
    return out[None]


def solution(mesh):
    placed = (P(("group", "tile"), None, None), P("group"), P(), P(), P(), P(), P())
    return jax.shard_map(
        per_device,
        mesh=mesh,
        in_specs=placed,
        out_specs=P(("group", "tile"), None, None, None, None),
        check_vma=False,
    )
```

```python
import functools

import jax
import jax.numpy as jnp
from jax import lax
from jax.experimental import pallas as pl
from jax.experimental.pallas import tpu as pltpu
from jax.sharding import PartitionSpec as P

WS = 16
TF = 2
LANES = 128
GAP = LANES // 2
WIDE = WS + 5
HALF = (WIDE + 1) // 2


def norm_act(x, gain):
    scale = lax.rsqrt(jnp.mean(x * x, axis=-1, keepdims=True) + 1e-06)
    h = x * scale * (0.5 * gain)
    return h + h * jnp.tanh(h)


def row_shift(x, by):
    rows = lax.broadcasted_iota(jnp.int32, x.shape, 0)
    n = x.shape[0]
    if by > 0:
        return jnp.where(rows == 0, 0.0, pltpu.roll(x, 1, 0))
    return jnp.where(rows == n - 1, 0.0, pltpu.roll(x, n - 1, 0))


def exchange_kernel(sizes, lat_hbm, got, lat_ref, pad_a, pad_b, packed, stage, send_sem, recv_sem, own_sem, lat_sem):
    tiles, strips, frames, shard_rows = sizes
    quarters = tiles // frames
    blocks = tiles // strips
    offset = strips // 2 - 1
    me = lax.axis_index("tile")
    fetch = pltpu.make_async_copy(lat_hbm, lat_ref, lat_sem)
    fetch.start()
    barrier = pltpu.get_barrier_semaphore()
    for step in range(1, tiles):
        pl.semaphore_signal(barrier, inc=1, device_id={"tile": lax.rem(me + step, tiles)})

    wl = lat_ref.shape[1]
    fetch.wait()
    values = lat_ref[...].astype(jnp.float32)
    spare = jnp.zeros((2 * LANES - values.shape[0], wl), jnp.float32)
    for pad, rows in ((pad_a, values[:LANES]), (pad_b, jnp.concatenate([values[LANES:], spare]))):
        pad[:8] = jnp.zeros((8, LANES), jnp.float32)
        pad[8 + wl :] = jnp.zeros((WS, LANES), jnp.float32)
        pad[8 : 8 + wl] = rows.T
    low = lax.broadcasted_iota(jnp.int32, (HALF, LANES), 1) < LANES // 2
    for s in range(strips):
        at = WS * s + 8 - 3
        packed[s, :WIDE] = pad_a[at : at + WIDE]
        upper = pltpu.roll(pad_b[at + HALF : at + 2 * HALF], LANES // 2, 1)
        packed[s, WIDE:] = jnp.where(low, pad_b[at : at + HALF], upper)
        stage[s] = packed[s].astype(jnp.bfloat16)
    pl.semaphore_wait(barrier, tiles - 1)

    frame = me // quarters
    quarter = me % quarters

    def each_send(act):
        for ahead in range(3):
            block = frame // TF + ahead
            slot = (2 * TF - TF * ahead + frame % TF) * quarters + quarter

            @pl.when(block < blocks)
            def _():
                @pl.loop(0, strips)
                def _(j):
                    s = (j + me) % strips
                    to = (block * strips + s + offset) % tiles

                    @pl.when(to != me)
                    def _():
                        act(
                            pltpu.make_async_remote_copy(
                                src_ref=stage.at[s],
                                dst_ref=got.at[slot],
                                send_sem=send_sem.at[ahead * strips + s],
                                recv_sem=recv_sem.at[slot],
                                device_id={"tile": to},
                            ),
                            None,
                        )

                    @pl.when(to == me)
                    def _():
                        act(None, pltpu.make_async_copy(stage.at[s], got.at[slot], own_sem))

    def start(remote, local):
        (remote if local is None else local).start()

    def finish(remote, local):
        if local is None:
            remote.wait_send()
        else:
            local.wait()

    each_send(start)
    mine = (me + tiles - offset) % tiles // strips

    @pl.loop(0, 3 * TF * quarters)
    def _(slot):
        source = (TF * mine - 2 * TF) * quarters + slot

        @pl.when(jnp.logical_and(source >= 0, source != me))
        def _():
            pltpu.make_async_remote_copy(
                src_ref=stage.at[0],
                dst_ref=got.at[slot],
                send_sem=send_sem.at[0],
                recv_sem=recv_sem.at[slot],
                device_id={"tile": me},
            ).wait_recv()

    each_send(finish)


def decode_kernel(
    sizes, clip, got_ref, w1_ref, g1_ref, wm_hbm, g2_ref, hw_ref, out_ref,
    wm, act, firstb, fscr, acc, outw, w1, main, tail, rowtap, z_ref, sem,
):
    tiles, strips, hl, clat, shard_rows = sizes
    ch = g1_ref.shape[-1]
    patch = hw_ref.shape[0] // 3
    half = patch // 2
    aw = WS + 3
    ow = WS + 1
    lanes = WS * half
    rotated = (lax.axis_index("tile") + tiles - (strips // 2 - 1)) % tiles
    strip = rotated % strips
    block = rotated // strips
    scal = []
    for i in range(3 * TF):
        at = block * TF - 2 * TF + i
        scal.append(jnp.where(at < 0, -1, clip[jnp.maximum(at, 0)]))
    g1 = g1_ref[...].reshape(1, ch)
    g2 = g2_ref[...].reshape(1, ch)

    def tap_copies(dt):
        return [
            pltpu.make_async_copy(
                wm_hbm.at[dt, dr, dc],
                wm.at[pl.ds(dc * ch, ch), pl.ds((3 * dt + dr) * ch, ch)],
                sem.at[dt],
            )
            for dr in range(3)
            for dc in range(3)
        ]

    for dt in (2, 1, 0):
        for copy in tap_copies(dt):
            copy.start()

    group = 3 * clat
    w1[...] = jnp.zeros_like(w1)
    for dt in range(3):
        for dr in range(3):
            w1[dt, dr * GAP : dr * GAP + group] = w1_ref[dt, dr * group : (dr + 1) * group]
    wide = rowtap.shape[0] // (hl + 2)
    rowtap[:wide] = jnp.zeros((wide, LANES), jnp.float32)
    rowtap[(hl + 1) * wide :] = jnp.zeros((wide, LANES), jnp.float32)
    at_lane = lax.broadcasted_iota(jnp.int32, (wide, LANES), 1)
    quarters = hl // shard_rows
    per = LANES // clat

    for f in range(3 * TF):

        @pl.when(block * TF - 2 * TF + f < 0)
        def _(f=f):
            z_ref[f] = jnp.zeros(z_ref.shape[1:], jnp.bfloat16)

        @pl.when(block * TF - 2 * TF + f >= 0)
        def _(f=f):
            for q in range(quarters):
                main[q] = got_ref[f * quarters + q].astype(jnp.float32)
                tail[q, :HALF] = main[q, WIDE:]
                tail[q, HALF : 2 * HALF] = pltpu.roll(main[q, WIDE:], LANES // 2, 1)
                for first_row, count, x in ((0, per, main.at[q]), (per, shard_rows - per, tail.at[q])):
                    shifts = [x[dc : dc + wide] for dc in range(3)]
                    for r in range(count):
                        y = jnp.zeros((wide, LANES), jnp.float32)
                        for dc in (2, 1, 0):
                            turn = (dc - r) * clat % LANES
                            moved = pltpu.roll(shifts[dc], turn, 1) if turn else shifts[dc]
                            y = jnp.where(at_lane < (dc + 1) * clat, moved, y)
                        start = (1 + q * shard_rows + first_row + r) * wide
                        rowtap[start : start + wide] = y

            for w in range(aw):
                v = [
                    rowtap[pl.ds(dr * wide + w, hl, stride=wide), :] for dr in range(3)
                ]
                low = v[0] + pltpu.roll(v[1], GAP, 1)
                z_ref[f, w, :, :LANES] = low.astype(jnp.bfloat16)
                z_ref[f, w, :, LANES:] = v[2].astype(jnp.bfloat16)

    for f in range(TF + 2):
        if f == 0:
            needed = scal[2] == scal[4]
        elif f == 1:
            needed = jnp.logical_or(scal[3] == scal[4], scal[3] == scal[5])
        else:
            needed = scal[4] == scal[4]

        @pl.when(needed)
        def _(f=f):
            taps = []
            for dt in range(3):
                keep = (scal[f + dt] == scal[f + 2]).astype(jnp.float32)
                lhs = z_ref[f + dt].reshape(aw * hl, z_ref.shape[-1])
                taps.append(lhs * keep.astype(jnp.bfloat16) if dt < 2 else lhs)
            fscr[...] = jnp.dot(
                jnp.concatenate(taps, axis=-1), w1[...].reshape(-1, ch),
                preferred_element_type=jnp.float32,
            ).reshape(aw, hl, ch)

            for w in range(aw):
                rounded = fscr[w].astype(jnp.bfloat16)
                if f >= 2:
                    firstb[f - 2, w] = rounded
                value = norm_act(rounded.astype(jnp.float32), g1)
                if w < 2:
                    value = value * (strip > 0).astype(jnp.float32)
                if w == aw - 1:
                    value = value * (strip < strips - 1).astype(jnp.float32)
                act[f, w] = value.astype(jnp.bfloat16)

    wide_out = 3 * ch

    def unit(f, start, count):
        lhs = jnp.concatenate(
            [act[f, pl.ds(dc, ow)].reshape(ow * hl, ch) for dc in range(3)], axis=-1
        )
        taps = wm[:, start * wide_out : (start + count) * wide_out]
        return jnp.dot(lhs, taps, preferred_element_type=jnp.float32)

    def arrived(dt):
        for copy in tap_copies(dt):
            copy.wait()

    arrived(2)
    acc[:, :wide_out] = unit(3, 2, 1)
    arrived(1)

    @pl.when(scal[4] == scal[5])
    def _():
        both = unit(2, 1, 2)
        acc[:, :wide_out] += both[:, :wide_out]
        acc[:, wide_out:] = both[:, wide_out:]

    @pl.when(scal[4] != scal[5])
    def _():
        acc[:, wide_out:] = unit(2, 2, 1)

    arrived(0)

    @pl.when(scal[3] == scal[5])
    def _():
        acc[...] += unit(1, 0, 2)

    @pl.when(jnp.logical_and(scal[3] == scal[4], scal[3] != scal[5]))
    def _():
        acc[:, wide_out:] += unit(1, 1, 1)

    @pl.when(scal[2] == scal[4])
    def _():
        acc[:, wide_out:] += unit(0, 0, 1)

    rows = lax.broadcasted_iota(jnp.int32, (3 * patch, 6 * lanes), 0)
    cols = lax.broadcasted_iota(jnp.int32, (3 * patch, 6 * lanes), 1)
    odd = cols // (3 * lanes)
    colour = (cols // lanes) % 3
    want = colour * patch + (cols % lanes + half * odd) % patch
    spread = (rows == want).astype(jnp.bfloat16)
    head = lax.dot_general(
        hw_ref[...], spread, (((0,), (0,)), ((), ())), preferred_element_type=jnp.float32
    ).astype(jnp.bfloat16)
    lane = lax.broadcasted_iota(jnp.int32, (hl, lanes), 1)

    for fo in range(TF):
        for w in range(ow):
            part = acc[w * hl : (w + 1) * hl, (1 - fo) * wide_out : (2 - fo) * wide_out]
            summed = (
                firstb[fo, w + 1].astype(jnp.float32)
                + row_shift(part[:, :ch], 1)
                + part[:, ch : 2 * ch]
                + row_shift(part[:, 2 * ch :], -1)
            )
            value = norm_act(summed, g2)
            if w == 0:
                value = value * (strip > 0).astype(jnp.float32)
            outw[fo, w % 2, w // 2] = value.astype(jnp.bfloat16)

        p_odd = jnp.dot(
            outw[fo, 0].reshape(-1, ch), head[:, 3 * lanes :], preferred_element_type=jnp.float32
        )
        p_even = jnp.dot(
            outw[fo, 1, : WS // 2].reshape(-1, ch), head[:, : 3 * lanes],
            preferred_element_type=jnp.float32,
        )
        for k in range(3):
            front = jnp.zeros((hl, lanes), jnp.float32)
            back = jnp.zeros((hl, lanes), jnp.float32)
            for i in range(WS // 2):
                piece = p_even[i * hl : (i + 1) * hl, k * lanes : (k + 1) * lanes]
                front = jnp.where(lane // patch == i, piece, front)
            for i in range(WS // 2 + 1):
                piece = p_odd[i * hl : (i + 1) * hl, k * lanes : (k + 1) * lanes]
                back = jnp.where((lane + half) // patch == i, piece, back)
            out_ref[fo, k] = front + back


def per_device(latents, clip_index, first_conv, first_gain, middle_conv, head_gain, head_weight):
    tiles = lax.axis_size("tile")
    shard_rows, clat, wl = latents.shape
    ch = first_gain.shape[0]
    frames = clip_index.shape[0]
    hl = tiles * shard_rows // frames
    strips = wl // WS
    half = head_weight.shape[1] // 6
    aw = WS + 3
    quarters = tiles // frames
    slots = 3 * TF * quarters
    got = pl.pallas_call(
        functools.partial(exchange_kernel, (tiles, strips, frames, shard_rows)),
        out_shape=jax.ShapeDtypeStruct((slots, WIDE + HALF, LANES), jnp.bfloat16),
        in_specs=[pl.BlockSpec(memory_space=pl.ANY)],
        out_specs=pl.BlockSpec(memory_space=pl.ANY),
        scratch_shapes=[
            pltpu.VMEM((shard_rows * clat, wl), jnp.bfloat16),
            pltpu.VMEM((8 + wl + WS, LANES), jnp.float32),
            pltpu.VMEM((8 + wl + WS, LANES), jnp.float32),
            pltpu.VMEM((strips, WIDE + HALF, LANES), jnp.float32),
            pltpu.VMEM((strips, WIDE + HALF, LANES), jnp.bfloat16),
            pltpu.SemaphoreType.DMA((3 * strips,)),
            pltpu.SemaphoreType.DMA((slots,)),
            pltpu.SemaphoreType.DMA,
            pltpu.SemaphoreType.DMA,
        ],
        compiler_params=pltpu.CompilerParams(collective_id=0, has_side_effects=True),
    )(latents.reshape(shard_rows * clat, wl))
    vm = pl.BlockSpec(memory_space=pltpu.VMEM)
    out = pl.pallas_call(
        functools.partial(decode_kernel, (tiles, strips, hl, clat, shard_rows)),
        out_shape=jax.ShapeDtypeStruct((TF, 3, hl, WS * half), jnp.float32),
        in_specs=[
            pl.BlockSpec(memory_space=pltpu.SMEM), vm, vm, vm,
            pl.BlockSpec(memory_space=pl.ANY), vm, vm,
        ],
        out_specs=vm,
        scratch_shapes=[
            pltpu.VMEM((3 * ch, 9 * ch), jnp.bfloat16),
            pltpu.VMEM((TF + 2, aw, hl, ch), jnp.bfloat16),
            pltpu.VMEM((TF, aw, hl, ch), jnp.bfloat16),
            pltpu.VMEM((aw, hl, ch), jnp.float32),
            pltpu.VMEM(((WS + 1) * hl, TF * 3 * ch), jnp.float32),
            pltpu.VMEM((TF, 2, WS // 2 + 1, hl, ch), jnp.bfloat16),
            pltpu.VMEM((3, 2 * LANES, ch), jnp.bfloat16),
            pltpu.VMEM((quarters, WIDE + HALF, LANES), jnp.float32),
            pltpu.VMEM((quarters, WIDE + HALF, LANES), jnp.float32),
            pltpu.VMEM(((hl + 2) * 24, LANES), jnp.float32),
            pltpu.VMEM((3 * TF, aw, hl, 2 * LANES), jnp.bfloat16),
            pltpu.SemaphoreType.DMA((3,)),
        ],
        compiler_params=pltpu.CompilerParams(vmem_limit_bytes=60 * 1024 * 1024),
    )(
        clip_index, got, first_conv.reshape(3, 9 * clat, ch), first_gain, middle_conv,
        head_gain, head_weight.T,
    )
    return out[None]


def solution(mesh):
    placed = (P(("group", "tile"), None, None), P("group"), P(), P(), P(), P(), P())
    return jax.shard_map(
        per_device,
        mesh=mesh,
        in_specs=placed,
        out_specs=P(("group", "tile"), None, None, None, None),
        check_vma=False,
    )
```
